32 devices in a mesh: grp: 2 (over y), slab: 4 (over z), orb: 2 (over x), rep: 2 (over core).
Axes of the slice: x: 2, y: 2, z: 4, core: 2. Of those that a mesh axis runs over, the one named last changes fastest.
Arguments:
- orbitals: bfloat16 [16, 32, 1024], P(('grp', 'slab', 'orb')), parts along dimension 0, may hold values from -6 to 6
- corners: int32 [16, 3], P('grp'), parts along dimension 0, may hold values from 0 to 191, as said below
- partners: int32 [16, 24], P(('grp', 'slab', 'orb')), parts along dimension 0, may hold values from -1 to 7, as said below
- kernel: float32 [32, 1024], replicated, may hold values from 0.05 to 5
Outputs:
- exchange_boxes: float32 [16, 32, 1024], P(('grp', 'slab', 'orb')), parts along dimension 0
- exchange_energy: float32 [2], P('grp'), parts along dimension 0
The draws below stay inside these ranges and needn't reach their ends.
There are 2 independent parts, one for each index of `grp`. The reference program is written for one: setup_inputs(seed, part) draws one part's arguments, and reference() takes and returns one part's arrays. A program takes and returns all parts, laid end to end along the dimension named above; an argument that names none is the same for every part. Nothing has to cross between parts.
Inputs may be any that keep to these rules, and one draw needn't show every extreme that they name: corners[i, 2] lies in the slab of orbital i: from 12 * (i // (1 * 2)) to 12 more less one; corners[i, 0] and corners[i, 1] lie below 192. `partners`: row i starts with i itself, names distinct orbitals whose boxes intersect box i (every component of o is above -32 and below 32), and has its -1 entries only after all others.
All inputs are finite; a program needn't handle non-finite values.
Results may differ from the reference program's by a relative error of at most 0.0003.
Values may be sent and summed in bfloat16 or wider, within the bound.
No kernel may reach another device: no remote copies, remote signals or barrier semaphores. Data moves between devices by JAX's collectives and lax.ppermute only.
A program may use at most 64 MiB of HBM per device.

```python
import math
import jax
import jax.numpy as jnp
from jax import lax

B = 32
G = 192
ZDEV = 12
ORB_DEV = 1
NB = 24
NORB = 8
N_SLAB = 4
N_ORB = 2


def pair_tables(key):
    orbital_count = NORB
    group_size = ORB_DEV * N_ORB
    ranked_count = min(NB, NORB)
    subkeys = jax.random.split(key, 5)
    orbital_ids = jnp.arange(orbital_count, dtype=jnp.int32)
    slab_ids = orbital_ids // group_size
    corner_x = jnp.mod(jax.random.randint(subkeys[0], (orbital_count,), -B, B), G)
    corner_y = jnp.mod(jax.random.randint(subkeys[1], (orbital_count,), -B, B), G)
    corner_z = slab_ids * ZDEV + jax.random.randint(subkeys[2], (orbital_count,), 0, ZDEV)
    corners = jnp.stack([corner_x, corner_y, corner_z], axis=1).astype(jnp.int32)
    lengths = jnp.array([G, G, ZDEV * N_SLAB], jnp.int32)
    deltas = corners[:, None, :] - corners[None, :, :]
    halfway = lengths // 2
    offsets = jnp.mod(deltas + halfway, lengths) - halfway
    intersection = jnp.all(jnp.abs(offsets) < B, axis=2)
    random_rank = jax.random.randint(subkeys[3], (orbital_count, orbital_count), 0, (1 << 29) // orbital_count)
    scores = jnp.where(intersection, 1 << 30, 0) + random_rank * orbital_count + orbital_ids[None, :]
    scores = jnp.where(orbital_ids[:, None] == orbital_ids[None, :], jnp.int32(2147483647), scores).astype(jnp.int32)
    ranked = lax.top_k(scores, ranked_count)[1].astype(jnp.int32)
    picked = jnp.take_along_axis(intersection, ranked, axis=1)
    if ranked_count < NB:
        ranked = jnp.concatenate([ranked, jnp.zeros((orbital_count, NB - ranked_count), jnp.int32)], axis=1)
        picked = jnp.concatenate([picked, jnp.zeros((orbital_count, NB - ranked_count), bool)], axis=1)
    filled = jax.random.randint(subkeys[4], (orbital_count, 1), 1, NB + 1)
    slot_ids = jnp.arange(NB, dtype=jnp.int32)[None, :]
    usable = (slot_ids < filled) & picked
    partners = jnp.where(usable, ranked, -1).astype(jnp.int32)
    return (corners, partners)


def draw_corners(key, part):
    return pair_tables(jax.random.fold_in(key, 11))[0]


def draw_partners(key, part):
    return pair_tables(jax.random.fold_in(key, 11))[1]


def levels(own_key, shape, pieces, least, high):
    factor_of, own = 1.0, jax.random.fold_in(own_key, 6)
    for position, blocks in pieces:
        steps = jnp.exp(jax.random.uniform(jax.random.fold_in(own, position), (blocks,), jnp.float32, least / len(pieces), high / len(pieces)))
        factor_of = factor_of * jnp.repeat(steps, shape[position] // blocks).reshape([-1 if axis == position else 1 for axis in range(len(shape))])
    return factor_of


def normal_values(own_key, shape, width, reach, shards=(), held_as=jnp.bfloat16):
    gain = levels(own_key, shape, shards, -0.22, 0.18) if shards else 1.0
    result = jax.random.normal(own_key, shape, jnp.float32) * width * gain
    return jnp.minimum(jnp.maximum(result, -reach), reach).astype(held_as)


def setup_inputs(seed: int = 0, part: int = 0) -> dict:
    arg_keys = jax.random.split(jax.random.key(seed), 5)
    own_keys = jax.random.split(jax.random.fold_in(arg_keys[4], part), 5)
    return {
        "orbitals": normal_values(own_keys[0], (NORB, B, B * B), 1.0, 6.0, ((0, 8),)),
        "corners": draw_corners(jax.random.fold_in(jax.random.fold_in(arg_keys[4], part), 71), part),
        "partners": draw_partners(jax.random.fold_in(jax.random.fold_in(arg_keys[4], part), 71), part),
        "kernel": jnp.clip(jnp.exp(jax.random.uniform(arg_keys[3], (B, B * B), jnp.float32, math.log(0.05), math.log(5.0))), 0.05, 5.0),
    }


def wrapped(deltas, lengths):
    halfway = lengths // 2
    return jnp.mod(deltas + halfway, lengths) - halfway


def reference(orbitals, corners, partners, kernel):
    box_edge = orbitals.shape[1]
    box_count = orbitals.shape[0]
    cube_view = orbitals.reshape(box_count, box_edge, box_edge, box_edge)
    spectrum = kernel.reshape(box_edge, box_edge, box_edge)
    lengths = jnp.array([G, G, ZDEV * N_SLAB], jnp.int32)

    def one_orbital(orbital_id):
        centre = cube_view[orbital_id].astype(jnp.float32)
        corner = corners[orbital_id]

        def single_pair(partner):
            usable = partner >= 0
            safe_id = jnp.maximum(partner, 0).astype(jnp.int32)
            offset = wrapped(corner - corners[safe_id], lengths).astype(jnp.int32)
            padded = jnp.pad(cube_view[safe_id].astype(jnp.float32), box_edge)
            anchor = (offset + box_edge).astype(jnp.int32)
            shifted = lax.dynamic_slice(padded, (anchor[0], anchor[1], anchor[2]), (box_edge, box_edge, box_edge))
            shifted = jnp.where(usable, shifted, jnp.zeros_like(shifted))
            density = centre * shifted
            potential = jnp.real(jnp.fft.ifftn(spectrum * jnp.fft.fftn(density)))
            return potential * shifted, jnp.sum(density * potential)

        pair_terms, energies = lax.map(single_pair, partners[orbital_id])
        return -jnp.sum(pair_terms, axis=0), jnp.sum(energies)

    exchange_boxes, energies = lax.map(one_orbital, jnp.arange(box_count, dtype=jnp.int32))
    exchange_energy = -jnp.sum(energies) / (2.0 * box_count * box_edge ** 3)
    return exchange_boxes.reshape(box_count, box_edge, box_edge * box_edge), exchange_energy.reshape(1)
```

```python
import functools

import jax
import jax.numpy as jnp
import numpy as np
from jax import lax
from jax.experimental import pallas as pl
from jax.experimental.pallas import tpu as pltpu
from jax.sharding import PartitionSpec as P

G = 192
ZDEV = 12
PB = 4
RADIX = 4


def passed_along(array, axis, by):
    size = lax.axis_size(axis)
    return lax.ppermute(array, axis, [(i, (i + by) % size) for i in range(size)])


def halves(table):
    table = np.asarray(table, np.float32)
    high = table.astype(jnp.bfloat16)
    low = (table - high.astype(np.float32)).astype(jnp.bfloat16)
    return np.stack([high, low])


def fourier_tables(box_edge):
    inner = box_edge // RADIX
    unit = 2.0 * np.pi / box_edge
    s, c, q1, r = np.meshgrid(
        np.arange(inner), np.arange(box_edge), np.arange(inner), np.arange(box_edge), indexing="ij"
    )
    tile = inner * box_edge
    plane = []
    for q0 in range(RADIX - 1):
        angle = (((q0 + RADIX * q1) * s + r * c) % box_edge).reshape(tile, tile) * unit
        plane.append(np.concatenate([np.cos(angle), -np.sin(angle)], axis=1))
    ids = np.arange(box_edge)
    edge_angle = (ids[:, None] * ids[None, :] % box_edge) * unit
    cosine = np.kron(np.eye(PB), np.cos(edge_angle))
    sine = np.kron(np.eye(PB), np.sin(edge_angle))
    ahead = np.block([[cosine, sine], [-sine, cosine]])
    return halves(np.stack(plane)), halves(np.stack([ahead, ahead.T]))


def split(values):
    high = values.astype(jnp.bfloat16)
    return high, (values - high.astype(jnp.float32)).astype(jnp.bfloat16)


def product(left, right, dims):
    one = functools.partial(
        lax.dot_general, dimension_numbers=(dims, ((), ())), preferred_element_type=jnp.float32
    )
    return one(left[0], right[0]) + (one(left[1], right[0]) + one(left[0], right[1]))


NN = ((1,), (0,))
NT = ((1,), (1,))


def pair_kernel(
    partners, corners, pool, own, filters, plane_tab, edge_tab, out, energy, moved_box,
    *, slab_count, orb_count, halo_depth, whole_pool
):
    own_count, box_edge, plane = own.shape
    slot_count = partners.shape[1]
    tile = plane // RADIX
    rows = PB * box_edge
    slab_position = lax.axis_index("slab")
    first_own = (slab_position * orb_count + lax.axis_index("orb")) * own_count
    group_size = own_count * orb_count
    lengths = (G, G, ZDEV * slab_count)
    a_ids = lax.broadcasted_iota(jnp.int32, (box_edge, 1), 0)
    lane_ids = lax.broadcasted_iota(jnp.int32, (1, plane), 1)
    b_ids = lane_ids // box_edge
    c_ids = lane_ids % box_edge
    total = jnp.zeros((1, 1), jnp.float32)
    for o in range(own_count):
        centre = own[o].astype(jnp.float32)
        filled = jnp.int32(0)
        for k in range(slot_count):
            filled = filled + (partners[o, k] >= 0).astype(jnp.int32)
        out[o] = jnp.zeros((box_edge, plane), jnp.float32)

        def block(step, carry):
            for p in range(PB):
                slot = step * PB + p
                partner = partners[o, jnp.minimum(slot, slot_count - 1)]
                usable = (partner >= 0) & (slot < slot_count)
                partner = jnp.maximum(partner, 0)
                shift = []
                for d in range(3):
                    half = lengths[d] // 2
                    delta = corners[first_own + o, d] - corners[partner, d] + half
                    delta = jnp.where(delta < 0, delta + lengths[d], delta)
                    delta = jnp.where(delta >= lengths[d], delta - lengths[d], delta)
                    shift.append(delta - half)
                if whole_pool:
                    row = partner
                else:
                    away = partner // group_size - slab_position + halo_depth
                    away = lax.rem(away + slab_count, slab_count)
                    row = away * group_size + lax.rem(partner, group_size)
                box = pool[row].astype(jnp.float32)
                flat = shift[1] * box_edge + shift[2]
                flat = lax.rem(RADIX * plane - flat, plane)
                box = pltpu.roll(box, flat, 1)
                box = pltpu.roll(box, lax.rem(RADIX * box_edge - shift[0], box_edge), 0)
                a_src = a_ids + shift[0]
                b_src = b_ids + shift[1]
                c_src = c_ids + shift[2]
                in_a = (a_src >= 0) & (a_src < box_edge) & usable
                in_bc = (b_src >= 0) & (b_src < box_edge) & (c_src >= 0) & (c_src < box_edge)
                weight = in_a.astype(jnp.float32) * in_bc.astype(jnp.float32)
                moved_box[p] = box * weight
            density = (moved_box[...] * centre[None]).reshape(rows, plane)
            x0, x1, x2, x3 = (density[:, t * tile:(t + 1) * tile] for t in range(RADIX))
            even, odd = x0 + x2, x1 + x3
            tables = [(plane_tab[0, q], plane_tab[1, q]) for q in range(RADIX - 1)]
            y0 = product(split(even + odd), tables[0], NN)
            y2 = product(split(even - odd), tables[2], NN)
            uv = product(split(jnp.concatenate([x0 - x2, x1 - x3], axis=0)), tables[1], NN)
            y1_re = uv[:rows, :tile] + uv[rows:, tile:]
            y1_im = uv[:rows, tile:] - uv[rows:, :tile]
            spectrum = jnp.concatenate(
                [
                    jnp.concatenate([y0[:, :tile], y1_re, y2[:, :tile]], axis=1),
                    jnp.concatenate([y0[:, tile:], y1_im, y2[:, tile:]], axis=1),
                ],
                axis=0,
            )
            spectrum = product((edge_tab[0, 0], edge_tab[1, 0]), split(spectrum), NN)
            width = spectrum.shape[1]
            spectrum = spectrum.reshape(2 * PB, box_edge, width) * filters[...][None]
            spectrum = spectrum.reshape(2 * rows, width)
            spectrum = product((edge_tab[0, 1], edge_tab[1, 1]), split(spectrum), NN)
            re, im = spectrum[:rows], spectrum[rows:]
            pick = lambda part, q: part[:, q * tile:(q + 1) * tile]
            z0 = product(split(jnp.concatenate([pick(re, 0), pick(im, 0)], axis=1)), tables[0], NT)
            z2 = product(split(jnp.concatenate([pick(re, 2), pick(im, 2)], axis=1)), tables[2], NT)
            both = jnp.concatenate(
                [
                    jnp.concatenate([pick(re, 1), pick(im, 1)], axis=1),
                    jnp.concatenate([pick(im, 1), -pick(re, 1)], axis=1),
                ],
                axis=0,
            )
            z1 = product(split(both), tables[1], NT)
            z1_re, z1_im = z1[:rows], z1[rows:]
            even, odd = z0 + z2, z0 - z2
            parts = (even + z1_re, odd - z1_im, even - z1_re, odd + z1_im)
            for t in range(RADIX):
                span = pl.ds(t * tile, tile)
                term = parts[t].reshape(PB, box_edge, tile) * moved_box[:, :, span]
                out[o, :, span] = out[o, :, span] - jnp.sum(term, axis=0)
            return carry

        lax.fori_loop(0, (filled + PB - 1) // PB, block, 0)
        summed = jnp.sum(out[o] * centre, axis=0, keepdims=True)
        total = total + jnp.sum(summed, axis=1, keepdims=True)
    energy[...] = total


def body(orbitals, corners, partners, kernel):
    own_count, box_edge, plane = orbitals.shape
    slab_count = lax.axis_size("slab")
    orb_count = lax.axis_size("orb")
    halo_depth = (ZDEV + box_edge - 2) // ZDEV
    whole_pool = slab_count <= 2 * halo_depth + 1
    if whole_pool:
        pool = lax.all_gather(orbitals, ("slab", "orb"), axis=0, tiled=True)
    else:
        gathered = lax.all_gather(orbitals, "orb", axis=0, tiled=True)
        lower = [gathered]
        upper = [gathered]
        for _ in range(halo_depth):
            lower.append(passed_along(lower[-1], "slab", 1))
            upper.append(passed_along(upper[-1], "slab", -1))
        pool = jnp.concatenate(lower[::-1] + upper[1:], axis=0)
    cube = kernel.reshape(box_edge, box_edge, box_edge) * (1.0 / box_edge**3)
    mirrored = jnp.roll(jnp.flip(cube, (0, 1, 2)), 1, (0, 1, 2))
    filters = jnp.concatenate(
        [cube[:, 0::RADIX], cube[:, 1::RADIX] + mirrored[:, 1::RADIX], cube[:, 2::RADIX]], axis=1
    ).reshape(box_edge, (RADIX - 1) * plane // RADIX)
    plane_tab, edge_tab = fourier_tables(box_edge)
    smem = pl.BlockSpec(memory_space=pltpu.SMEM)
    vmem = pl.BlockSpec(memory_space=pltpu.VMEM)
    exchange, energy = pl.pallas_call(
        functools.partial(
            pair_kernel,
            slab_count=slab_count,
            orb_count=orb_count,
            halo_depth=halo_depth,
            whole_pool=whole_pool,
        ),
        in_specs=[smem, smem, vmem, vmem, vmem, vmem, vmem],
        out_specs=[vmem, vmem],
        out_shape=[
            jax.ShapeDtypeStruct((own_count, box_edge, plane), jnp.float32),
            jax.ShapeDtypeStruct((1, 1), jnp.float32),
        ],
        scratch_shapes=[pltpu.VMEM((PB, box_edge, plane), jnp.float32)],
        name="pairs",
    )(partners, corners, pool, orbitals, filters, plane_tab, edge_tab)
    energy_all = lax.psum(energy.reshape(1), ("slab", "orb"))
    orbital_total = own_count * slab_count * orb_count
    return exchange, energy_all / (2.0 * orbital_total * box_edge**3)


def solution(mesh):
    in_specs = (
        P(("grp", "slab", "orb"), None, None),
        P("grp", None),
        P(("grp", "slab", "orb"), None),
        P(),
    )
    out_specs = (P(("grp", "slab", "orb"), None, None), P("grp"))
    return jax.shard_map(body, mesh=mesh, in_specs=in_specs, out_specs=out_specs, check_vma=False)
```

```python
import functools
import math

import jax
import jax.numpy as jnp
import numpy as np
from jax import lax
from jax.experimental import pallas as pl
from jax.experimental.pallas import tpu as pltpu
from jax.sharding import PartitionSpec as P

G = 192
ZDEV = 12
PB = 4
RADIX = 4


def passed_along(array, axis, by):
    size = lax.axis_size(axis)
    return lax.ppermute(array, axis, [(i, (i + by) % size) for i in range(size)])


def swapped_sum(value, axes):
    size = math.prod(lax.axis_size(axis) for axis in axes)
    if size & (size - 1) or size > 4:
        return lax.psum(value, axes)
    terms = [value] + [
        lax.ppermute(value, axes, [(i, i ^ d) for i in range(size)]) for d in range(1, size)
    ]
    while len(terms) > 1:
        terms = [terms[i] + terms[i + 1] for i in range(0, len(terms), 2)]
    return terms[0]


def turned_boxes(orbitals):
    axes = ("slab", "orb", "rep")
    slabs, side = lax.axis_size("slab"), lax.axis_size("orb")
    boxes = []
    for d in range(slabs):
        moves = [
            ((s * side + x) * side + r, ((s + d) % slabs * side + r) * side + x)
            for s in range(slabs)
            for x in range(side)
            for r in range(side)
        ]
        boxes.append(lax.ppermute(orbitals, axes, moves))
    return boxes


def halves(table):
    table = np.asarray(table, np.float32)
    high = table.astype(jnp.bfloat16)
    low = (table - high.astype(np.float32)).astype(jnp.bfloat16)
    return np.stack([high, low])


def fourier_tables(box_edge):
    inner = box_edge // RADIX
    unit = 2.0 * np.pi / box_edge
    s, c, q1, r = np.meshgrid(
        np.arange(inner), np.arange(box_edge), np.arange(inner), np.arange(box_edge), indexing="ij"
    )
    tile = inner * box_edge
    plane = []
    for q0 in range(RADIX - 1):
        angle = (((q0 + RADIX * q1) * s + r * c) % box_edge).reshape(tile, tile) * unit
        plane.append(np.concatenate([np.cos(angle), -np.sin(angle)], axis=1))
    ids = np.arange(box_edge)
    edge_angle = (ids[:, None] * ids[None, :] % box_edge) * unit
    cosine = np.kron(np.eye(PB), np.cos(edge_angle))
    sine = np.kron(np.eye(PB), np.sin(edge_angle))
    ahead = np.block([[cosine, sine], [-sine, cosine]])
    return halves(np.stack(plane)), halves(np.stack([ahead, ahead.T]))


def split(values):
    high = values.astype(jnp.bfloat16)
    return high, (values - high.astype(jnp.float32)).astype(jnp.bfloat16)


def product(left, right, dims):
    one = functools.partial(
        lax.dot_general, dimension_numbers=(dims, ((), ())), preferred_element_type=jnp.float32
    )
    return one(left[0], right[0]) + (one(left[1], right[0]) + one(left[0], right[1]))


NN = ((1,), (0,))
NT = ((1,), (1,))


def pair_kernel(*refs, slab_count, orb_count, rep_count, halo_depth, turned):
    partners, corners, own, filters, plane_tab, edge_tab = refs[:6]
    pools = refs[6:-4]
    out, energy, moved_box, chosen = refs[-4:]
    own_count, box_edge, plane = own.shape
    slot_count = partners.shape[1]
    tile = plane // RADIX
    rows = PB * box_edge
    slab_position = lax.axis_index("slab")
    first_own = (slab_position * orb_count + lax.axis_index("orb")) * own_count
    group_size = own_count * orb_count
    lengths = (G, G, ZDEV * slab_count)
    a_ids = lax.broadcasted_iota(jnp.int32, (box_edge, 1), 0)
    lane_ids = lax.broadcasted_iota(jnp.int32, (1, plane), 1)
    b_ids = lane_ids // box_edge
    c_ids = lane_ids % box_edge
    total = jnp.zeros((1, 1), jnp.float32)
    for o in range(own_count):
        centre = own[o].astype(jnp.float32)
        filled = jnp.int32(0)
        for k in range(slot_count):
            partner = partners[o, k]
            column = lax.rem(jnp.maximum(partner, 0) // own_count, orb_count)
            mine = (partner >= 0) & (lax.rem(column, rep_count) == lax.axis_index("rep"))
            chosen[filled] = partner
            filled = filled + mine.astype(jnp.int32)
        out[o] = jnp.zeros((box_edge, plane), jnp.float32)

        def block(step, carry):
            for p in range(PB):
                slot = step * PB + p
                usable = slot < filled
                partner = jnp.where(usable, chosen[jnp.minimum(slot, slot_count - 1)], 0)
                shift = []
                for d in range(3):
                    half = lengths[d] // 2
                    delta = corners[first_own + o, d] - corners[partner, d] + half
                    delta = jnp.where(delta < 0, delta + lengths[d], delta)
                    delta = jnp.where(delta >= lengths[d], delta - lengths[d], delta)
                    shift.append(delta - half)
                slab = partner // group_size
                if turned:
                    away = lax.rem(slab_position - slab + slab_count, slab_count)
                    inner = lax.rem(partner, own_count)
                    box = pools[0][inner]
                    for d in range(1, slab_count):
                        box = jnp.where(away == d, pools[d][inner], box)
                else:
                    away = lax.rem(slab - slab_position + halo_depth + slab_count, slab_count)
                    box = pools[0][away * group_size + lax.rem(partner, group_size)]
                box = box.astype(jnp.float32)
                flat = shift[1] * box_edge + shift[2]
                flat = lax.rem(RADIX * plane - flat, plane)
                box = pltpu.roll(box, flat, 1)
                box = pltpu.roll(box, lax.rem(RADIX * box_edge - shift[0], box_edge), 0)
                a_src = a_ids + shift[0]
                b_src = b_ids + shift[1]
                c_src = c_ids + shift[2]
                in_a = (a_src >= 0) & (a_src < box_edge) & usable
                in_bc = (b_src >= 0) & (b_src < box_edge) & (c_src >= 0) & (c_src < box_edge)
                weight = in_a.astype(jnp.float32) * in_bc.astype(jnp.float32)
                moved_box[p] = box * weight
            density = (moved_box[...] * centre[None]).reshape(rows, plane)
            x0, x1, x2, x3 = (density[:, t * tile:(t + 1) * tile] for t in range(RADIX))
            even, odd = x0 + x2, x1 + x3
            tables = [(plane_tab[0, q], plane_tab[1, q]) for q in range(RADIX - 1)]
            y0 = product(split(even + odd), tables[0], NN)
            y2 = product(split(even - odd), tables[2], NN)
            uv = product(split(jnp.concatenate([x0 - x2, x1 - x3], axis=0)), tables[1], NN)
            y1_re = uv[:rows, :tile] + uv[rows:, tile:]
            y1_im = uv[:rows, tile:] - uv[rows:, :tile]
            spectrum = jnp.concatenate(
                [
                    jnp.concatenate([y0[:, :tile], y1_re, y2[:, :tile]], axis=1),
                    jnp.concatenate([y0[:, tile:], y1_im, y2[:, tile:]], axis=1),
                ],
                axis=0,
            )
            spectrum = product((edge_tab[0, 0], edge_tab[1, 0]), split(spectrum), NN)
            width = spectrum.shape[1]
            spectrum = spectrum.reshape(2 * PB, box_edge, width) * filters[...][None]
            spectrum = spectrum.reshape(2 * rows, width)
            spectrum = product((edge_tab[0, 1], edge_tab[1, 1]), split(spectrum), NN)
            re, im = spectrum[:rows], spectrum[rows:]
            pick = lambda part, q: part[:, q * tile:(q + 1) * tile]
            z0 = product(split(jnp.concatenate([pick(re, 0), pick(im, 0)], axis=1)), tables[0], NT)
            z2 = product(split(jnp.concatenate([pick(re, 2), pick(im, 2)], axis=1)), tables[2], NT)
            both = jnp.concatenate(
                [
                    jnp.concatenate([pick(re, 1), pick(im, 1)], axis=1),
                    jnp.concatenate([pick(im, 1), -pick(re, 1)], axis=1),
                ],
                axis=0,
            )
            z1 = product(split(both), tables[1], NT)
            z1_re, z1_im = z1[:rows], z1[rows:]
            even, odd = z0 + z2, z0 - z2
            parts = (even + z1_re, odd - z1_im, even - z1_re, odd + z1_im)
            for t in range(RADIX):
                span = pl.ds(t * tile, tile)
                term = parts[t].reshape(PB, box_edge, tile) * moved_box[:, :, span]
                out[o, :, span] = out[o, :, span] - jnp.sum(term, axis=0)
            return carry

        lax.fori_loop(0, (filled + PB - 1) // PB, block, 0)
        summed = jnp.sum(out[o] * centre, axis=0, keepdims=True)
        total = total + jnp.sum(summed, axis=1, keepdims=True)
    energy[...] = total


def body(orbitals, corners, partners, kernel):
    own_count, box_edge, plane = orbitals.shape
    slab_count = lax.axis_size("slab")
    orb_count = lax.axis_size("orb")
    halo_depth = (ZDEV + box_edge - 2) // ZDEV
    rep_count = lax.axis_size("rep")
    turned = slab_count <= 2 * halo_depth + 1 and orb_count == rep_count
    if turned:
        pools = turned_boxes(orbitals)
    else:
        gathered = lax.all_gather(orbitals, "orb", axis=0, tiled=True)
        lower = [gathered]
        upper = [gathered]
        for _ in range(halo_depth):
            lower.append(passed_along(lower[-1], "slab", 1))
            upper.append(passed_along(upper[-1], "slab", -1))
        pools = [jnp.concatenate(lower[::-1] + upper[1:], axis=0)]
    cube = kernel.reshape(box_edge, box_edge, box_edge) * (1.0 / box_edge**3)
    mirrored = jnp.roll(jnp.flip(cube, (0, 1, 2)), 1, (0, 1, 2))
    filters = jnp.concatenate(
        [cube[:, 0::RADIX], cube[:, 1::RADIX] + mirrored[:, 1::RADIX], cube[:, 2::RADIX]], axis=1
    ).reshape(box_edge, (RADIX - 1) * plane // RADIX)
    plane_tab, edge_tab = fourier_tables(box_edge)
    smem = pl.BlockSpec(memory_space=pltpu.SMEM)
    vmem = pl.BlockSpec(memory_space=pltpu.VMEM)
    exchange, energy = pl.pallas_call(
        functools.partial(
            pair_kernel,
            slab_count=slab_count,
            orb_count=orb_count,
            rep_count=rep_count,
            halo_depth=halo_depth,
            turned=turned,
        ),
        in_specs=[smem, smem, vmem, vmem, vmem, vmem] + [vmem] * len(pools),
        out_specs=[vmem, vmem],
        out_shape=[
            jax.ShapeDtypeStruct((own_count, box_edge, plane), jnp.float32),
            jax.ShapeDtypeStruct((1, 1), jnp.float32),
        ],
        scratch_shapes=[
            pltpu.VMEM((PB, box_edge, plane), jnp.float32),
            pltpu.SMEM((partners.shape[1] + 1,), jnp.int32),
        ],
        name="pairs",
    )(partners, corners, orbitals, filters, plane_tab, edge_tab, *pools)
    exchange = swapped_sum(exchange, ("rep",))
    energy_all = swapped_sum(swapped_sum(energy.reshape(1), ("slab",)), ("orb", "rep"))
    orbital_total = own_count * slab_count * orb_count
    return exchange, energy_all / (2.0 * orbital_total * box_edge**3)


def solution(mesh):
    in_specs = (
        P(("grp", "slab", "orb"), None, None),
        P("grp", None),
        P(("grp", "slab", "orb"), None),
        P(),
    )
    out_specs = (P(("grp", "slab", "orb"), None, None), P("grp"))
    return jax.shard_map(body, mesh=mesh, in_specs=in_specs, out_specs=out_specs, check_vma=False)
```

```python
import functools
import math

import jax
import jax.numpy as jnp
import numpy as np
from jax import lax
from jax.experimental import pallas as pl
from jax.experimental.pallas import tpu as pltpu
from jax.sharding import PartitionSpec as P

G = 192
ZDEV = 12
PB = 4
RADIX = 4


def passed_along(array, axis, by):
    size = lax.axis_size(axis)
    return lax.ppermute(array, axis, [(i, (i + by) % size) for i in range(size)])


def swapped_sum(value, axes):
    for axis in axes:
        size = lax.axis_size(axis)
        if size & (size - 1):
            value = lax.psum(value, axis)
            continue
        step = 1
        while step < size:
            value = value + lax.ppermute(value, axis, [(i, i ^ step) for i in range(size)])
            step *= 2
    return value


def turned_boxes(orbitals):
    axes = ("slab", "orb", "rep")
    slabs, side = lax.axis_size("slab"), lax.axis_size("orb")
    boxes = []
    for d in range(slabs):
        moves = [
            ((s * side + x) * side + r, ((s + d) % slabs * side + r) * side + x)
            for s in range(slabs)
            for x in range(side)
            for r in range(side)
        ]
        boxes.append(lax.ppermute(orbitals, axes, moves))
    return boxes


def halves(table):
    table = np.asarray(table, np.float32)
    high = table.astype(jnp.bfloat16)
    low = (table - high.astype(np.float32)).astype(jnp.bfloat16)
    return np.stack([high, low])


def fourier_tables(box_edge):
    inner = box_edge // RADIX
    unit = 2.0 * np.pi / box_edge
    s, c, q1, r = np.meshgrid(
        np.arange(inner), np.arange(box_edge), np.arange(inner), np.arange(box_edge), indexing="ij"
    )
    tile = inner * box_edge
    plane = []
    for q0 in range(RADIX - 1):
        angle = (((q0 + RADIX * q1) * s + r * c) % box_edge).reshape(tile, tile) * unit
        plane.append(np.concatenate([np.cos(angle), -np.sin(angle)], axis=1))
    ids = np.arange(box_edge)
    edge_angle = (ids[:, None] * ids[None, :] % box_edge) * unit
    cosine = np.kron(np.eye(PB), np.cos(edge_angle))
    sine = np.kron(np.eye(PB), np.sin(edge_angle))
    ahead = np.block([[cosine, sine], [-sine, cosine]])
    return halves(np.stack(plane)), halves(np.stack([ahead, ahead.T]))


def split(values):
    high = values.astype(jnp.bfloat16)
    return high, (values - high.astype(jnp.float32)).astype(jnp.bfloat16)


def product(left, right, dims):
    one = functools.partial(
        lax.dot_general, dimension_numbers=(dims, ((), ())), preferred_element_type=jnp.float32
    )
    return one(left[0], right[0]) + (one(left[1], right[0]) + one(left[0], right[1]))


NN = ((1,), (0,))
NT = ((1,), (1,))


def one_hot(source, target):
    return (source == target).astype(jnp.float32).astype(jnp.bfloat16)


def moved_by(left, right):
    return jnp.dot(left, right, preferred_element_type=jnp.float32)


def ordered_filters(kernel):
    box_edge, plane = kernel.shape
    tile, inner = plane // RADIX, box_edge // RADIX
    high, rest = split(kernel)
    rest = kernel - high.astype(jnp.float32)
    mid, low = split(rest)
    pieces = jnp.concatenate([high, mid, low], axis=0)
    count = pieces.shape[0]
    stacked = jnp.concatenate([pieces[:, t * tile:(t + 1) * tile] for t in range(RADIX)], axis=0)
    source = lax.broadcasted_iota(jnp.int32, (tile, tile), 0)
    target = lax.broadcasted_iota(jnp.int32, (tile, tile), 1)
    share = tile // RADIX
    within = target % share
    decimated = (target // share + RADIX * (within // box_edge)) * box_edge + within % box_edge
    stacked = moved_by(stacked, one_hot(source, decimated))
    groups = [
        jnp.concatenate(
            [
                stacked[t * count:(t + 1) * count, q * share:(q + 1) * share]
                for t in range(RADIX)
            ],
            axis=1,
        )
        for q in range(RADIX)
    ]
    back = (inner - 1 - target // box_edge) * box_edge + (box_edge - target % box_edge) % box_edge
    mirrored = moved_by(groups[3].astype(jnp.bfloat16), one_hot(source, back))
    rows = lax.broadcasted_iota(jnp.int32, (count, count), 0)
    cols = lax.broadcasted_iota(jnp.int32, (count, count), 1)
    opposite = rows // box_edge * box_edge + (box_edge - rows % box_edge) % box_edge
    mirrored = moved_by(one_hot(opposite, cols), mirrored.astype(jnp.bfloat16))

    def joined(group):
        return group[:box_edge] + group[box_edge:2 * box_edge] + group[2 * box_edge:]

    parts = [joined(groups[0]), joined(groups[1]) + joined(mirrored), joined(groups[2])]
    return jnp.concatenate(parts, axis=1) * (1.0 / box_edge**3)


def pair_kernel(*refs, slab_count, orb_count, rep_count, halo_depth, turned):
    partners, corners, own, kernel, plane_tab, edge_tab = refs[:6]
    pools = refs[6:-4]
    out, moved_box, filters, chosen = refs[-4:]
    own_count, box_edge, plane = own.shape
    slot_count = partners.shape[1]
    tile = plane // RADIX
    rows = PB * box_edge
    slab_position = lax.axis_index("slab")
    first_own = (slab_position * orb_count + lax.axis_index("orb")) * own_count
    group_size = own_count * orb_count
    lengths = (G, G, ZDEV * slab_count)
    a_ids = lax.broadcasted_iota(jnp.int32, (box_edge, 1), 0)
    lane_ids = lax.broadcasted_iota(jnp.int32, (1, plane), 1)
    b_ids = lane_ids // box_edge
    c_ids = lane_ids % box_edge
    total = jnp.zeros((1, 1), jnp.float32)
    filters[...] = ordered_filters(kernel[...])
    for o in range(own_count):
        centre = own[o].astype(jnp.float32)
        filled = jnp.int32(0)
        for k in range(slot_count):
            partner = partners[o, k]
            column = lax.rem(jnp.maximum(partner, 0) // own_count, orb_count)
            mine = (partner >= 0) & (lax.rem(column, rep_count) == lax.axis_index("rep"))
            chosen[filled] = partner
            filled = filled + mine.astype(jnp.int32)
        held = pl.ds(o * box_edge, box_edge)
        out[held] = jnp.zeros((box_edge, plane), jnp.float32)

        def block(step, carry):
            for p in range(PB):
                slot = step * PB + p
                usable = slot < filled
                partner = jnp.where(usable, chosen[jnp.minimum(slot, slot_count - 1)], 0)
                shift = []
                for d in range(3):
                    half = lengths[d] // 2
                    delta = corners[d, first_own + o] - corners[d, partner] + half
                    delta = jnp.where(delta < 0, delta + lengths[d], delta)
                    delta = jnp.where(delta >= lengths[d], delta - lengths[d], delta)
                    shift.append(delta - half)
                slab = partner // group_size
                if turned:
                    away = lax.rem(slab_position - slab + slab_count, slab_count)
                    inner = lax.rem(partner, own_count)
                    box = pools[0][inner]
                    for d in range(1, slab_count):
                        box = jnp.where(away == d, pools[d][inner], box)
                else:
                    away = lax.rem(slab - slab_position + halo_depth + slab_count, slab_count)
                    box = pools[0][away * group_size + lax.rem(partner, group_size)]
                box = box.astype(jnp.float32)
                flat = shift[1] * box_edge + shift[2]
                flat = lax.rem(RADIX * plane - flat, plane)
                box = pltpu.roll(box, flat, 1)
                box = pltpu.roll(box, lax.rem(RADIX * box_edge - shift[0], box_edge), 0)
                a_src = a_ids + shift[0]
                b_src = b_ids + shift[1]
                c_src = c_ids + shift[2]
                in_a = (a_src >= 0) & (a_src < box_edge) & usable
                in_bc = (b_src >= 0) & (b_src < box_edge) & (c_src >= 0) & (c_src < box_edge)
                weight = in_a.astype(jnp.float32) * in_bc.astype(jnp.float32)
                moved_box[p] = box * weight
            density = (moved_box[...] * centre[None]).reshape(rows, plane)
            x0, x1, x2, x3 = (density[:, t * tile:(t + 1) * tile] for t in range(RADIX))
            even, odd = x0 + x2, x1 + x3
            tables = [(plane_tab[0, q], plane_tab[1, q]) for q in range(RADIX - 1)]
            y0 = product(split(even + odd), tables[0], NN)
            y2 = product(split(even - odd), tables[2], NN)
            uv = product(split(jnp.concatenate([x0 - x2, x1 - x3], axis=0)), tables[1], NN)
            y1_re = uv[:rows, :tile] + uv[rows:, tile:]
            y1_im = uv[:rows, tile:] - uv[rows:, :tile]
            spectrum = jnp.concatenate(
                [
                    jnp.concatenate([y0[:, :tile], y1_re, y2[:, :tile]], axis=1),
                    jnp.concatenate([y0[:, tile:], y1_im, y2[:, tile:]], axis=1),
                ],
                axis=0,
            )
            spectrum = product((edge_tab[0, 0], edge_tab[1, 0]), split(spectrum), NN)
            width = spectrum.shape[1]
            spectrum = spectrum.reshape(2 * PB, box_edge, width) * filters[...][None]
            spectrum = spectrum.reshape(2 * rows, width)
            spectrum = product((edge_tab[0, 1], edge_tab[1, 1]), split(spectrum), NN)
            re, im = spectrum[:rows], spectrum[rows:]
            pick = lambda part, q: part[:, q * tile:(q + 1) * tile]
            z0 = product(split(jnp.concatenate([pick(re, 0), pick(im, 0)], axis=1)), tables[0], NT)
            z2 = product(split(jnp.concatenate([pick(re, 2), pick(im, 2)], axis=1)), tables[2], NT)
            both = jnp.concatenate(
                [
                    jnp.concatenate([pick(re, 1), pick(im, 1)], axis=1),
                    jnp.concatenate([pick(im, 1), -pick(re, 1)], axis=1),
                ],
                axis=0,
            )
            z1 = product(split(both), tables[1], NT)
            z1_re, z1_im = z1[:rows], z1[rows:]
            even, odd = z0 + z2, z0 - z2
            parts = (even + z1_re, odd - z1_im, even - z1_re, odd + z1_im)
            for t in range(RADIX):
                span = pl.ds(t * tile, tile)
                term = parts[t].reshape(PB, box_edge, tile) * moved_box[:, :, span]
                out[held, span] = out[held, span] - jnp.sum(term, axis=0)
            return carry

        lax.fori_loop(0, (filled + PB - 1) // PB, block, 0)
        summed = jnp.sum(out[held] * centre, axis=0, keepdims=True)
        total = total + jnp.sum(summed, axis=1, keepdims=True)
    out[pl.ds(own_count * box_edge, 8)] = jnp.broadcast_to(total, (8, plane))


def body(orbitals, corners, partners, kernel):
    own_count, box_edge, plane = orbitals.shape
    slab_count = lax.axis_size("slab")
    orb_count = lax.axis_size("orb")
    halo_depth = (ZDEV + box_edge - 2) // ZDEV
    rep_count = lax.axis_size("rep")
    turned = slab_count <= 2 * halo_depth + 1 and orb_count == rep_count
    if turned:
        pools = turned_boxes(orbitals)
    else:
        gathered = lax.all_gather(orbitals, "orb", axis=0, tiled=True)
        lower = [gathered]
        upper = [gathered]
        for _ in range(halo_depth):
            lower.append(passed_along(lower[-1], "slab", 1))
            upper.append(passed_along(upper[-1], "slab", -1))
        pools = [jnp.concatenate(lower[::-1] + upper[1:], axis=0)]
    plane_tab, edge_tab = fourier_tables(box_edge)
    smem = pl.BlockSpec(memory_space=pltpu.SMEM)
    vmem = pl.BlockSpec(memory_space=pltpu.VMEM)
    sums = pl.pallas_call(
        functools.partial(
            pair_kernel,
            slab_count=slab_count,
            orb_count=orb_count,
            rep_count=rep_count,
            halo_depth=halo_depth,
            turned=turned,
        ),
        in_specs=[smem, smem, vmem, vmem, vmem, vmem] + [vmem] * len(pools),
        out_specs=vmem,
        out_shape=jax.ShapeDtypeStruct((own_count * box_edge + 8, plane), jnp.float32),
        scratch_shapes=[
            pltpu.VMEM((PB, box_edge, plane), jnp.float32),
            pltpu.VMEM((box_edge, (RADIX - 1) * plane // RADIX), jnp.float32),
            pltpu.SMEM((partners.shape[1] + 1,), jnp.int32),
        ],
        name="pairs",
    )(partners, corners.T, orbitals, kernel, plane_tab, edge_tab, *pools)
    held = own_count * box_edge
    other = lax.ppermute(sums, "rep", [(i, i ^ 1) for i in range(rep_count)])
    energy = sums[held:, :128] + other[held:, :128]
    exchange = (sums[:held] + other[:held]).reshape(own_count, box_edge, plane)
    energy_all = swapped_sum(energy, ("orb", "slab"))[0, :1]
    orbital_total = own_count * slab_count * orb_count
    return exchange, energy_all / (2.0 * orbital_total * box_edge**3)


def solution(mesh):
    in_specs = (
        P(("grp", "slab", "orb"), None, None),
        P("grp", None),
        P(("grp", "slab", "orb"), None),
        P(),
    )
    out_specs = (P(("grp", "slab", "orb"), None, None), P("grp"))
    return jax.shard_map(body, mesh=mesh, in_specs=in_specs, out_specs=out_specs, check_vma=False)
```

```python
import functools
import math

import jax
import jax.numpy as jnp
import numpy as np
from jax import lax
from jax.experimental import pallas as pl
from jax.experimental.pallas import tpu as pltpu
from jax.sharding import PartitionSpec as P

G = 192
ZDEV = 12
PB = 4
RADIX = 4


def passed_along(array, axis, by):
    size = lax.axis_size(axis)
    return lax.ppermute(array, axis, [(i, (i + by) % size) for i in range(size)])


def swapped_sum(value, axes):
    for axis in axes:
        size = lax.axis_size(axis)
        if size & (size - 1):
            value = lax.psum(value, axis)
            continue
        step = 1
        while step < size:
            value = value + lax.ppermute(value, axis, [(i, i ^ step) for i in range(size)])
            step *= 2
    return value


def turned_boxes(orbitals):
    axes = ("slab", "orb", "rep")
    slabs, side = lax.axis_size("slab"), lax.axis_size("orb")
    moves = [
        ((s * side + x) * side + r, (s * side + r) * side + x)
        for s in range(slabs)
        for x in range(side)
        for r in range(side)
    ]
    turned = lax.ppermute(orbitals, axes, moves)
    boxes = {0: turned}
    for d in sorted(range(1, slabs), key=lambda d: -min(d, slabs - d)):
        boxes[d] = passed_along(turned, "slab", d)
    return [boxes[d] for d in range(slabs)]


def halves(table):
    table = np.asarray(table, np.float32)
    high = table.astype(jnp.bfloat16)
    low = (table - high.astype(np.float32)).astype(jnp.bfloat16)
    return np.stack([high, low])


def fourier_tables(box_edge):
    inner = box_edge // RADIX
    unit = 2.0 * np.pi / box_edge
    s, c, q1, r = np.meshgrid(
        np.arange(inner), np.arange(box_edge), np.arange(inner), np.arange(box_edge), indexing="ij"
    )
    tile = inner * box_edge
    plane = []
    for q0 in range(RADIX - 1):
        angle = (((q0 + RADIX * q1) * s + r * c) % box_edge).reshape(tile, tile) * unit
        plane.append(np.concatenate([np.cos(angle), -np.sin(angle)], axis=1))
    ids = np.arange(box_edge)
    edge_angle = (ids[:, None] * ids[None, :] % box_edge) * unit
    cosine = np.kron(np.eye(PB), np.cos(edge_angle))
    sine = np.kron(np.eye(PB), np.sin(edge_angle))
    ahead = np.block([[cosine, sine], [-sine, cosine]])
    return halves(np.stack(plane)), halves(np.stack([ahead, ahead.T]))


def split(values):
    high = values.astype(jnp.bfloat16)
    return high, (values - high.astype(jnp.float32)).astype(jnp.bfloat16)


def product(left, right, dims):
    one = functools.partial(
        lax.dot_general, dimension_numbers=(dims, ((), ())), preferred_element_type=jnp.float32
    )
    return one(left[0], right[0]) + (one(left[1], right[0]) + one(left[0], right[1]))


NN = ((1,), (0,))
NT = ((1,), (1,))


def one_hot(source, target):
    return (source == target).astype(jnp.float32).astype(jnp.bfloat16)


def moved_by(left, right):
    return jnp.dot(left, right, preferred_element_type=jnp.float32)


def ordered_filters(kernel):
    box_edge, plane = kernel.shape
    tile, inner = plane // RADIX, box_edge // RADIX
    high, rest = split(kernel)
    rest = kernel - high.astype(jnp.float32)
    mid, low = split(rest)
    pieces = jnp.concatenate([high, mid, low], axis=0)
    count = pieces.shape[0]
    stacked = jnp.concatenate([pieces[:, t * tile:(t + 1) * tile] for t in range(RADIX)], axis=0)
    source = lax.broadcasted_iota(jnp.int32, (tile, tile), 0)
    target = lax.broadcasted_iota(jnp.int32, (tile, tile), 1)
    share = tile // RADIX
    within = target % share
    decimated = (target // share + RADIX * (within // box_edge)) * box_edge + within % box_edge
    stacked = moved_by(stacked, one_hot(source, decimated))
    groups = [
        jnp.concatenate(
            [
                stacked[t * count:(t + 1) * count, q * share:(q + 1) * share]
                for t in range(RADIX)
            ],
            axis=1,
        )
        for q in range(RADIX)
    ]
    back = (inner - 1 - target // box_edge) * box_edge + (box_edge - target % box_edge) % box_edge
    mirrored = moved_by(groups[3].astype(jnp.bfloat16), one_hot(source, back))
    rows = lax.broadcasted_iota(jnp.int32, (count, count), 0)
    cols = lax.broadcasted_iota(jnp.int32, (count, count), 1)
    opposite = rows // box_edge * box_edge + (box_edge - rows % box_edge) % box_edge
    mirrored = moved_by(one_hot(opposite, cols), mirrored.astype(jnp.bfloat16))

    def joined(group):
        return group[:box_edge] + group[box_edge:2 * box_edge] + group[2 * box_edge:]

    parts = [joined(groups[0]), joined(groups[1]) + joined(mirrored), joined(groups[2])]
    return jnp.concatenate(parts, axis=1) * (1.0 / box_edge**3)


def pair_kernel(*refs, slab_count, orb_count, rep_count, halo_depth, turned):
    partners, corners, own, kernel, plane_source, edge_source = refs[:6]
    pools = refs[6:-7]
    out, moved_box, filters, chosen, plane_tab, edge_tab, arrived = refs[-7:]
    plane_copy = pltpu.make_async_copy(plane_source, plane_tab, arrived.at[0])
    edge_copy = pltpu.make_async_copy(edge_source, edge_tab, arrived.at[1])
    plane_copy.start()
    edge_copy.start()
    own_count, box_edge, plane = own.shape
    slot_count = partners.shape[1]
    tile = plane // RADIX
    rows = PB * box_edge
    slab_position = lax.axis_index("slab")
    first_own = (slab_position * orb_count + lax.axis_index("orb")) * own_count
    group_size = own_count * orb_count
    lengths = (G, G, ZDEV * slab_count)
    a_ids = lax.broadcasted_iota(jnp.int32, (box_edge, 1), 0)
    lane_ids = lax.broadcasted_iota(jnp.int32, (1, plane), 1)
    b_ids = lane_ids // box_edge
    c_ids = lane_ids % box_edge
    total = jnp.zeros((1, 1), jnp.float32)
    filters[...] = ordered_filters(kernel[...])
    plane_copy.wait()
    edge_copy.wait()
    for o in range(own_count):
        centre = own[o].astype(jnp.float32)
        filled = jnp.int32(0)
        for k in range(slot_count):
            partner = partners[o, k]
            column = lax.rem(jnp.maximum(partner, 0) // own_count, orb_count)
            mine = (partner >= 0) & (lax.rem(column, rep_count) == lax.axis_index("rep"))
            chosen[filled] = partner
            filled = filled + mine.astype(jnp.int32)
        held = pl.ds(o * box_edge, box_edge)
        out[held] = jnp.zeros((box_edge, plane), jnp.float32)

        def block(step, carry):
            for p in range(PB):
                slot = step * PB + p
                usable = slot < filled
                partner = jnp.where(usable, chosen[jnp.minimum(slot, slot_count - 1)], 0)
                shift = []
                for d in range(3):
                    half = lengths[d] // 2
                    delta = corners[d, first_own + o] - corners[d, partner] + half
                    delta = jnp.where(delta < 0, delta + lengths[d], delta)
                    delta = jnp.where(delta >= lengths[d], delta - lengths[d], delta)
                    shift.append(delta - half)
                slab = partner // group_size
                if turned:
                    away = lax.rem(slab_position - slab + slab_count, slab_count)
                    inner = lax.rem(partner, own_count)
                    box = pools[0][inner]
                    for d in range(1, slab_count):
                        box = jnp.where(away == d, pools[d][inner], box)
                else:
                    away = lax.rem(slab - slab_position + halo_depth + slab_count, slab_count)
                    box = pools[0][away * group_size + lax.rem(partner, group_size)]
                box = box.astype(jnp.float32)
                flat = shift[1] * box_edge + shift[2]
                flat = lax.rem(RADIX * plane - flat, plane)
                box = pltpu.roll(box, flat, 1)
                box = pltpu.roll(box, lax.rem(RADIX * box_edge - shift[0], box_edge), 0)
                a_src = a_ids + shift[0]
                b_src = b_ids + shift[1]
                c_src = c_ids + shift[2]
                in_a = (a_src >= 0) & (a_src < box_edge) & usable
                in_bc = (b_src >= 0) & (b_src < box_edge) & (c_src >= 0) & (c_src < box_edge)
                weight = in_a.astype(jnp.float32) * in_bc.astype(jnp.float32)
                moved_box[p] = box * weight
            density = (moved_box[...] * centre[None]).reshape(rows, plane)
            x0, x1, x2, x3 = (density[:, t * tile:(t + 1) * tile] for t in range(RADIX))
            even, odd = x0 + x2, x1 + x3
            tables = [(plane_tab[0, q], plane_tab[1, q]) for q in range(RADIX - 1)]
            y0 = product(split(even + odd), tables[0], NN)
            y2 = product(split(even - odd), tables[2], NN)
            uv = product(split(jnp.concatenate([x0 - x2, x1 - x3], axis=0)), tables[1], NN)
            y1_re = uv[:rows, :tile] + uv[rows:, tile:]
            y1_im = uv[:rows, tile:] - uv[rows:, :tile]
            spectrum = jnp.concatenate(
                [
                    jnp.concatenate([y0[:, :tile], y1_re, y2[:, :tile]], axis=1),
                    jnp.concatenate([y0[:, tile:], y1_im, y2[:, tile:]], axis=1),
                ],
                axis=0,
            )
            spectrum = product((edge_tab[0, 0], edge_tab[1, 0]), split(spectrum), NN)
            width = spectrum.shape[1]
            spectrum = spectrum.reshape(2 * PB, box_edge, width) * filters[...][None]
            spectrum = spectrum.reshape(2 * rows, width)
            spectrum = product((edge_tab[0, 1], edge_tab[1, 1]), split(spectrum), NN)
            re, im = spectrum[:rows], spectrum[rows:]
            pick = lambda part, q: part[:, q * tile:(q + 1) * tile]
            z0 = product(split(jnp.concatenate([pick(re, 0), pick(im, 0)], axis=1)), tables[0], NT)
            z2 = product(split(jnp.concatenate([pick(re, 2), pick(im, 2)], axis=1)), tables[2], NT)
            both = jnp.concatenate(
                [
                    jnp.concatenate([pick(re, 1), pick(im, 1)], axis=1),
                    jnp.concatenate([pick(im, 1), -pick(re, 1)], axis=1),
                ],
                axis=0,
            )
            z1 = product(split(both), tables[1], NT)
            z1_re, z1_im = z1[:rows], z1[rows:]
            even, odd = z0 + z2, z0 - z2
            parts = (even + z1_re, odd - z1_im, even - z1_re, odd + z1_im)
            for t in range(RADIX):
                span = pl.ds(t * tile, tile)
                term = parts[t].reshape(PB, box_edge, tile) * moved_box[:, :, span]
                out[held, span] = out[held, span] - jnp.sum(term, axis=0)
            return carry

        lax.fori_loop(0, (filled + PB - 1) // PB, block, 0)
        summed = jnp.sum(out[held] * centre, axis=0, keepdims=True)
        total = total + jnp.sum(summed, axis=1, keepdims=True)
    out[pl.ds(own_count * box_edge, 8)] = jnp.broadcast_to(total, (8, plane))


def body(orbitals, corners, partners, kernel):
    own_count, box_edge, plane = orbitals.shape
    slab_count = lax.axis_size("slab")
    orb_count = lax.axis_size("orb")
    halo_depth = (ZDEV + box_edge - 2) // ZDEV
    rep_count = lax.axis_size("rep")
    turned = slab_count <= 2 * halo_depth + 1 and orb_count == rep_count
    if turned:
        pools = turned_boxes(orbitals)
    else:
        gathered = lax.all_gather(orbitals, "orb", axis=0, tiled=True)
        lower = [gathered]
        upper = [gathered]
        for _ in range(halo_depth):
            lower.append(passed_along(lower[-1], "slab", 1))
            upper.append(passed_along(upper[-1], "slab", -1))
        pools = [jnp.concatenate(lower[::-1] + upper[1:], axis=0)]
    plane_tab, edge_tab = fourier_tables(box_edge)
    smem = pl.BlockSpec(memory_space=pltpu.SMEM)
    vmem = pl.BlockSpec(memory_space=pltpu.VMEM)
    whole = pl.BlockSpec(memory_space=pl.ANY)
    sums = pl.pallas_call(
        functools.partial(
            pair_kernel,
            slab_count=slab_count,
            orb_count=orb_count,
            rep_count=rep_count,
            halo_depth=halo_depth,
            turned=turned,
        ),
        in_specs=[smem, smem, vmem, vmem, whole, whole] + [vmem] * len(pools),
        out_specs=vmem,
        out_shape=jax.ShapeDtypeStruct((own_count * box_edge + 8, plane), jnp.float32),
        scratch_shapes=[
            pltpu.VMEM((PB, box_edge, plane), jnp.float32),
            pltpu.VMEM((box_edge, (RADIX - 1) * plane // RADIX), jnp.float32),
            pltpu.SMEM((partners.shape[1] + 1,), jnp.int32),
            pltpu.VMEM(plane_tab.shape, jnp.bfloat16),
            pltpu.VMEM(edge_tab.shape, jnp.bfloat16),
            pltpu.SemaphoreType.DMA((2,)),
        ],
        name="pairs",
    )(partners, corners.T, orbitals, kernel, plane_tab, edge_tab, *pools)
    held = own_count * box_edge
    other = lax.ppermute(sums, "rep", [(i, i ^ 1) for i in range(rep_count)])
    energy = sums[held:, :128] + other[held:, :128]
    exchange = (sums[:held] + other[:held]).reshape(own_count, box_edge, plane)
    energy_all = swapped_sum(energy, ("orb", "slab"))[0, :1]
    orbital_total = own_count * slab_count * orb_count
    return exchange, energy_all / (2.0 * orbital_total * box_edge**3)


def solution(mesh):
    in_specs = (
        P(("grp", "slab", "orb"), None, None),
        P("grp", None),
        P(("grp", "slab", "orb"), None),
        P(),
    )
    out_specs = (P(("grp", "slab", "orb"), None, None), P("grp"))
    return jax.shard_map(body, mesh=mesh, in_specs=in_specs, out_specs=out_specs, check_vma=False)
```

```python
import functools
import math

import jax
import jax.numpy as jnp
import numpy as np
from jax import lax
from jax.experimental import pallas as pl
from jax.experimental.pallas import tpu as pltpu
from jax.sharding import PartitionSpec as P

G = 192
ZDEV = 12
PB = 4
RADIX = 4


def passed_along(array, axis, by):
    size = lax.axis_size(axis)
    return lax.ppermute(array, axis, [(i, (i + by) % size) for i in range(size)])


def swapped_sum(value, axes):
    for axis in axes:
        size = lax.axis_size(axis)
        if size & (size - 1):
            value = lax.psum(value, axis)
            continue
        step = 1
        while step < size:
            value = value + lax.ppermute(value, axis, [(i, i ^ step) for i in range(size)])
            step *= 2
    return value


def turned_boxes(orbitals):
    axes = ("slab", "orb", "rep")
    slabs, side = lax.axis_size("slab"), lax.axis_size("orb")
    boxes = {}
    for d in sorted(range(slabs), key=lambda d: -min(d, slabs - d)):
        moves = [
            ((s * side + x) * side + r, ((s + d) % slabs * side + r) * side + x)
            for s in range(slabs)
            for x in range(side)
            for r in range(side)
        ]
        boxes[d] = lax.ppermute(orbitals, axes, moves)
    return [boxes[d] for d in range(slabs)]


def halves(table):
    table = np.asarray(table, np.float32)
    high = table.astype(jnp.bfloat16)
    low = (table - high.astype(np.float32)).astype(jnp.bfloat16)
    return np.stack([high, low])


def fourier_tables(box_edge):
    inner = box_edge // RADIX
    unit = 2.0 * np.pi / box_edge
    s, c, q1, r = np.meshgrid(
        np.arange(inner), np.arange(box_edge), np.arange(inner), np.arange(box_edge), indexing="ij"
    )
    tile = inner * box_edge
    plane = []
    for q0 in range(RADIX - 1):
        angle = (((q0 + RADIX * q1) * s + r * c) % box_edge).reshape(tile, tile) * unit
        plane.append(np.concatenate([np.cos(angle), -np.sin(angle)], axis=1))
    ids = np.arange(box_edge)
    edge_angle = (ids[:, None] * ids[None, :] % box_edge) * unit
    cosine = np.kron(np.eye(PB), np.cos(edge_angle))
    sine = np.kron(np.eye(PB), np.sin(edge_angle))
    ahead = np.block([[cosine, sine], [-sine, cosine]])
    return halves(np.stack(plane)), halves(np.stack([ahead, ahead.T]))


def split(values):
    high = values.astype(jnp.bfloat16)
    return high, (values - high.astype(jnp.float32)).astype(jnp.bfloat16)


def product(left, right, dims):
    one = functools.partial(
        lax.dot_general, dimension_numbers=(dims, ((), ())), preferred_element_type=jnp.float32
    )
    return one(left[0], right[0]) + (one(left[1], right[0]) + one(left[0], right[1]))


NN = ((1,), (0,))
NT = ((1,), (1,))


def one_hot(source, target):
    return (source == target).astype(jnp.float32).astype(jnp.bfloat16)


def moved_by(left, right):
    return jnp.dot(left, right, preferred_element_type=jnp.float32)


def ordered_filters(kernel):
    box_edge, plane = kernel.shape
    tile, inner = plane // RADIX, box_edge // RADIX
    high, rest = split(kernel)
    rest = kernel - high.astype(jnp.float32)
    mid, low = split(rest)
    pieces = jnp.concatenate([high, mid, low], axis=0)
    count = pieces.shape[0]
    stacked = jnp.concatenate([pieces[:, t * tile:(t + 1) * tile] for t in range(RADIX)], axis=0)
    source = lax.broadcasted_iota(jnp.int32, (tile, tile), 0)
    target = lax.broadcasted_iota(jnp.int32, (tile, tile), 1)
    share = tile // RADIX
    within = target % share
    decimated = (target // share + RADIX * (within // box_edge)) * box_edge + within % box_edge
    stacked = moved_by(stacked, one_hot(source, decimated))
    groups = [
        jnp.concatenate(
            [
                stacked[t * count:(t + 1) * count, q * share:(q + 1) * share]
                for t in range(RADIX)
            ],
            axis=1,
        )
        for q in range(RADIX)
    ]
    back = (inner - 1 - target // box_edge) * box_edge + (box_edge - target % box_edge) % box_edge
    mirrored = moved_by(groups[3].astype(jnp.bfloat16), one_hot(source, back))
    rows = lax.broadcasted_iota(jnp.int32, (count, count), 0)
    cols = lax.broadcasted_iota(jnp.int32, (count, count), 1)
    opposite = rows // box_edge * box_edge + (box_edge - rows % box_edge) % box_edge
    mirrored = moved_by(one_hot(opposite, cols), mirrored.astype(jnp.bfloat16))

    def joined(group):
        return group[:box_edge] + group[box_edge:2 * box_edge] + group[2 * box_edge:]

    parts = [joined(groups[0]), joined(groups[1]) + joined(mirrored), joined(groups[2])]
    return jnp.concatenate(parts, axis=1) * (1.0 / box_edge**3)


def pair_kernel(*refs, slab_count, orb_count, rep_count, halo_depth, turned):
    partners, corners, own, kernel, plane_tab, edge_tab = refs[:6]
    pools = refs[6:-4]
    out, moved_box, filters, chosen = refs[-4:]
    own_count, box_edge, plane = own.shape
    slot_count = partners.shape[1]
    tile = plane // RADIX
    rows = PB * box_edge
    slab_position = lax.axis_index("slab")
    first_own = (slab_position * orb_count + lax.axis_index("orb")) * own_count
    group_size = own_count * orb_count
    lengths = (G, G, ZDEV * slab_count)
    a_ids = lax.broadcasted_iota(jnp.int32, (box_edge, 1), 0)
    lane_ids = lax.broadcasted_iota(jnp.int32, (1, plane), 1)
    b_ids = lane_ids // box_edge
    c_ids = lane_ids % box_edge
    total = jnp.zeros((1, 1), jnp.float32)
    filters[...] = ordered_filters(kernel[...])
    for o in range(own_count):
        centre = own[o].astype(jnp.float32)
        filled = jnp.int32(0)
        for k in range(slot_count):
            partner = partners[o, k]
            column = lax.rem(jnp.maximum(partner, 0) // own_count, orb_count)
            mine = (partner >= 0) & (lax.rem(column, rep_count) == lax.axis_index("rep"))
            chosen[filled] = partner
            filled = filled + mine.astype(jnp.int32)
        held = pl.ds(o * box_edge, box_edge)
        out[held] = jnp.zeros((box_edge, plane), jnp.float32)

        def block(step, carry):
            for p in range(PB):
                slot = step * PB + p
                usable = slot < filled
                partner = jnp.where(usable, chosen[jnp.minimum(slot, slot_count - 1)], 0)
                shift = []
                for d in range(3):
                    half = lengths[d] // 2
                    delta = corners[d, first_own + o] - corners[d, partner] + half
                    delta = jnp.where(delta < 0, delta + lengths[d], delta)
                    delta = jnp.where(delta >= lengths[d], delta - lengths[d], delta)
                    shift.append(delta - half)
                slab = partner // group_size
                if turned:
                    away = lax.rem(slab_position - slab + slab_count, slab_count)
                    inner = lax.rem(partner, own_count)
                    box = pools[0][inner]
                    for d in range(1, slab_count):
                        box = jnp.where(away == d, pools[d][inner], box)
                else:
                    away = lax.rem(slab - slab_position + halo_depth + slab_count, slab_count)
                    box = pools[0][away * group_size + lax.rem(partner, group_size)]
                box = box.astype(jnp.float32)
                flat = shift[1] * box_edge + shift[2]
                flat = lax.rem(RADIX * plane - flat, plane)
                box = pltpu.roll(box, flat, 1)
                box = pltpu.roll(box, lax.rem(RADIX * box_edge - shift[0], box_edge), 0)
                a_src = a_ids + shift[0]
                b_src = b_ids + shift[1]
                c_src = c_ids + shift[2]
                in_a = (a_src >= 0) & (a_src < box_edge) & usable
                in_bc = (b_src >= 0) & (b_src < box_edge) & (c_src >= 0) & (c_src < box_edge)
                weight = in_a.astype(jnp.float32) * in_bc.astype(jnp.float32)
                moved_box[p] = box * weight
            density = (moved_box[...] * centre[None]).reshape(rows, plane)
            x0, x1, x2, x3 = (density[:, t * tile:(t + 1) * tile] for t in range(RADIX))
            even, odd = x0 + x2, x1 + x3
            tables = [(plane_tab[0, q], plane_tab[1, q]) for q in range(RADIX - 1)]
            y0 = product(split(even + odd), tables[0], NN)
            y2 = product(split(even - odd), tables[2], NN)
            uv = product(split(jnp.concatenate([x0 - x2, x1 - x3], axis=0)), tables[1], NN)
            y1_re = uv[:rows, :tile] + uv[rows:, tile:]
            y1_im = uv[:rows, tile:] - uv[rows:, :tile]
            spectrum = jnp.concatenate(
                [
                    jnp.concatenate([y0[:, :tile], y1_re, y2[:, :tile]], axis=1),
                    jnp.concatenate([y0[:, tile:], y1_im, y2[:, tile:]], axis=1),
                ],
                axis=0,
            )
            spectrum = product((edge_tab[0, 0], edge_tab[1, 0]), split(spectrum), NN)
            width = spectrum.shape[1]
            spectrum = spectrum.reshape(2 * PB, box_edge, width) * filters[...][None]
            spectrum = spectrum.reshape(2 * rows, width)
            spectrum = product((edge_tab[0, 1], edge_tab[1, 1]), split(spectrum), NN)
            re, im = spectrum[:rows], spectrum[rows:]
            pick = lambda part, q: part[:, q * tile:(q + 1) * tile]
            z0 = product(split(jnp.concatenate([pick(re, 0), pick(im, 0)], axis=1)), tables[0], NT)
            z2 = product(split(jnp.concatenate([pick(re, 2), pick(im, 2)], axis=1)), tables[2], NT)
            both = jnp.concatenate(
                [
                    jnp.concatenate([pick(re, 1), pick(im, 1)], axis=1),
                    jnp.concatenate([pick(im, 1), -pick(re, 1)], axis=1),
                ],
                axis=0,
            )
            z1 = product(split(both), tables[1], NT)
            z1_re, z1_im = z1[:rows], z1[rows:]
            even, odd = z0 + z2, z0 - z2
            parts = (even + z1_re, odd - z1_im, even - z1_re, odd + z1_im)
            for t in range(RADIX):
                span = pl.ds(t * tile, tile)
                term = parts[t].reshape(PB, box_edge, tile) * moved_box[:, :, span]
                out[held, span] = out[held, span] - jnp.sum(term, axis=0)
            return carry

        lax.fori_loop(0, (filled + PB - 1) // PB, block, 0)
        summed = jnp.sum(out[held] * centre, axis=0, keepdims=True)
        total = total + jnp.sum(summed, axis=1, keepdims=True)
    out[pl.ds(own_count * box_edge, 8)] = jnp.broadcast_to(total, (8, plane))


def body(orbitals, corners, partners, kernel):
    own_count, box_edge, plane = orbitals.shape
    slab_count = lax.axis_size("slab")
    orb_count = lax.axis_size("orb")
    halo_depth = (ZDEV + box_edge - 2) // ZDEV
    rep_count = lax.axis_size("rep")
    turned = slab_count <= 2 * halo_depth + 1 and orb_count == rep_count
    if turned:
        pools = turned_boxes(orbitals)
    else:
        gathered = lax.all_gather(orbitals, "orb", axis=0, tiled=True)
        lower = [gathered]
        upper = [gathered]
        for _ in range(halo_depth):
            lower.append(passed_along(lower[-1], "slab", 1))
            upper.append(passed_along(upper[-1], "slab", -1))
        pools = [jnp.concatenate(lower[::-1] + upper[1:], axis=0)]
    plane_tab, edge_tab = fourier_tables(box_edge)
    smem = pl.BlockSpec(memory_space=pltpu.SMEM)
    vmem = pl.BlockSpec(memory_space=pltpu.VMEM)
    sums = pl.pallas_call(
        functools.partial(
            pair_kernel,
            slab_count=slab_count,
            orb_count=orb_count,
            rep_count=rep_count,
            halo_depth=halo_depth,
            turned=turned,
        ),
        in_specs=[smem, smem, vmem, vmem, vmem, vmem] + [vmem] * len(pools),
        out_specs=vmem,
        out_shape=jax.ShapeDtypeStruct((own_count * box_edge + 8, plane), jnp.float32),
        scratch_shapes=[
            pltpu.VMEM((PB, box_edge, plane), jnp.float32),
            pltpu.VMEM((box_edge, (RADIX - 1) * plane // RADIX), jnp.float32),
            pltpu.SMEM((partners.shape[1] + 1,), jnp.int32),
        ],
        name="pairs",
    )(partners, corners.T, orbitals, kernel, plane_tab, edge_tab, *pools)
    held = own_count * box_edge
    other = lax.ppermute(sums, "rep", [(i, i ^ 1) for i in range(rep_count)])
    energy = sums[held:, :128] + other[held:, :128]
    exchange = (sums[:held] + other[:held]).reshape(own_count, box_edge, plane)
    energy_all = swapped_sum(energy, ("orb", "slab"))[0, :1]
    orbital_total = own_count * slab_count * orb_count
    return exchange, energy_all / (2.0 * orbital_total * box_edge**3)


def solution(mesh):
    in_specs = (
        P(("grp", "slab", "orb"), None, None),
        P("grp", None),
        P(("grp", "slab", "orb"), None),
        P(),
    )
    out_specs = (P(("grp", "slab", "orb"), None, None), P("grp"))
    return jax.shard_map(body, mesh=mesh, in_specs=in_specs, out_specs=out_specs, check_vma=False)
```

```python
import functools
import math

import jax
import jax.numpy as jnp
import numpy as np
from jax import lax
from jax.experimental import pallas as pl
from jax.experimental.pallas import tpu as pltpu
from jax.sharding import PartitionSpec as P

G = 192
ZDEV = 12
PB = 4
RADIX = 4


def passed_along(array, axis, by):
    size = lax.axis_size(axis)
    return lax.ppermute(array, axis, [(i, (i + by) % size) for i in range(size)])


def swapped_sum(value, axes):
    for axis in axes:
        size = lax.axis_size(axis)
        if size & (size - 1):
            value = lax.psum(value, axis)
            continue
        if size == 4:
            first, second, third = (
                lax.ppermute(value, axis, [(i, i ^ d) for i in range(size)]) for d in (1, 2, 3)
            )
            value = (value + first) + (second + third)
            continue
        step = 1
        while step < size:
            value = value + lax.ppermute(value, axis, [(i, i ^ step) for i in range(size)])
            step *= 2
    return value


def turned_boxes(orbitals):
    axes = ("slab", "orb", "rep")
    slabs, side = lax.axis_size("slab"), lax.axis_size("orb")
    boxes = []
    for d in range(slabs):
        moves = [
            ((s * side + x) * side + r, ((s + d) % slabs * side + r) * side + x)
            for s in range(slabs)
            for x in range(side)
            for r in range(side)
        ]
        boxes.append(lax.ppermute(orbitals, axes, moves))
    return boxes


def halves(table):
    table = np.asarray(table, np.float32)
    high = table.astype(jnp.bfloat16)
    low = (table - high.astype(np.float32)).astype(jnp.bfloat16)
    return np.stack([high, low])


def fourier_tables(box_edge):
    inner = box_edge // RADIX
    unit = 2.0 * np.pi / box_edge
    s, c, q1, r = np.meshgrid(
        np.arange(inner), np.arange(box_edge), np.arange(inner), np.arange(box_edge), indexing="ij"
    )
    tile = inner * box_edge
    plane = []
    for q0 in range(RADIX - 1):
        angle = (((q0 + RADIX * q1) * s + r * c) % box_edge).reshape(tile, tile) * unit
        plane.append(np.concatenate([np.cos(angle), -np.sin(angle)], axis=1))
    ids = np.arange(box_edge)
    edge_angle = (ids[:, None] * ids[None, :] % box_edge) * unit
    cosine = np.kron(np.eye(PB), np.cos(edge_angle))
    sine = np.kron(np.eye(PB), np.sin(edge_angle))
    ahead = np.block([[cosine, sine], [-sine, cosine]])
    return halves(np.stack(plane)), halves(np.stack([ahead, ahead.T]))


def split(values):
    high = values.astype(jnp.bfloat16)
    return high, (values - high.astype(jnp.float32)).astype(jnp.bfloat16)


def product(left, right, dims):
    one = functools.partial(
        lax.dot_general, dimension_numbers=(dims, ((), ())), preferred_element_type=jnp.float32
    )
    return one(left[0], right[0]) + (one(left[1], right[0]) + one(left[0], right[1]))


NN = ((1,), (0,))
NT = ((1,), (1,))


def one_hot(source, target):
    return (source == target).astype(jnp.float32).astype(jnp.bfloat16)


def moved_by(left, right):
    return jnp.dot(left, right, preferred_element_type=jnp.float32)


def ordered_filters(kernel):
    box_edge, plane = kernel.shape
    tile, inner = plane // RADIX, box_edge // RADIX
    high, rest = split(kernel)
    rest = kernel - high.astype(jnp.float32)
    mid, low = split(rest)
    pieces = jnp.concatenate([high, mid, low], axis=0)
    count = pieces.shape[0]
    stacked = jnp.concatenate([pieces[:, t * tile:(t + 1) * tile] for t in range(RADIX)], axis=0)
    source = lax.broadcasted_iota(jnp.int32, (tile, tile), 0)
    target = lax.broadcasted_iota(jnp.int32, (tile, tile), 1)
    share = tile // RADIX
    within = target % share
    decimated = (target // share + RADIX * (within // box_edge)) * box_edge + within % box_edge
    stacked = moved_by(stacked, one_hot(source, decimated))
    groups = [
        jnp.concatenate(
            [
                stacked[t * count:(t + 1) * count, q * share:(q + 1) * share]
                for t in range(RADIX)
            ],
            axis=1,
        )
        for q in range(RADIX)
    ]
    back = (inner - 1 - target // box_edge) * box_edge + (box_edge - target % box_edge) % box_edge
    mirrored = moved_by(groups[3].astype(jnp.bfloat16), one_hot(source, back))
    rows = lax.broadcasted_iota(jnp.int32, (count, count), 0)
    cols = lax.broadcasted_iota(jnp.int32, (count, count), 1)
    opposite = rows // box_edge * box_edge + (box_edge - rows % box_edge) % box_edge
    mirrored = moved_by(one_hot(opposite, cols), mirrored.astype(jnp.bfloat16))

    def joined(group):
        return group[:box_edge] + group[box_edge:2 * box_edge] + group[2 * box_edge:]

    parts = [joined(groups[0]), joined(groups[1]) + joined(mirrored), joined(groups[2])]
    return jnp.concatenate(parts, axis=1) * (1.0 / box_edge**3)


def pair_kernel(*refs, slab_count, orb_count, rep_count, halo_depth, turned):
    partners, corners, own, kernel, plane_tab, edge_tab = refs[:6]
    pools = refs[6:-4]
    out, moved_box, filters, chosen = refs[-4:]
    own_count, box_edge, plane = own.shape
    slot_count = partners.shape[1]
    tile = plane // RADIX
    rows = PB * box_edge
    slab_position = lax.axis_index("slab")
    first_own = (slab_position * orb_count + lax.axis_index("orb")) * own_count
    group_size = own_count * orb_count
    lengths = (G, G, ZDEV * slab_count)
    a_ids = lax.broadcasted_iota(jnp.int32, (box_edge, 1), 0)
    lane_ids = lax.broadcasted_iota(jnp.int32, (1, plane), 1)
    b_ids = lane_ids // box_edge
    c_ids = lane_ids % box_edge
    total = jnp.zeros((1, 1), jnp.float32)
    filters[...] = ordered_filters(kernel[...])
    for o in range(own_count):
        centre = own[o].astype(jnp.float32)
        filled = jnp.int32(0)
        for k in range(slot_count):
            partner = partners[o, k]
            column = lax.rem(jnp.maximum(partner, 0) // own_count, orb_count)
            mine = (partner >= 0) & (lax.rem(column, rep_count) == lax.axis_index("rep"))
            chosen[filled] = partner
            filled = filled + mine.astype(jnp.int32)
        held = pl.ds(o * box_edge, box_edge)
        out[held] = jnp.zeros((box_edge, plane), jnp.float32)

        def block(step, carry):
            for p in range(PB):
                slot = step * PB + p
                usable = slot < filled
                partner = jnp.where(usable, chosen[jnp.minimum(slot, slot_count - 1)], 0)
                shift = []
                for d in range(3):
                    half = lengths[d] // 2
                    delta = corners[d, first_own + o] - corners[d, partner] + half
                    delta = jnp.where(delta < 0, delta + lengths[d], delta)
                    delta = jnp.where(delta >= lengths[d], delta - lengths[d], delta)
                    shift.append(delta - half)
                slab = partner // group_size
                if turned:
                    away = lax.rem(slab_position - slab + slab_count, slab_count)
                    inner = lax.rem(partner, own_count)
                    box = pools[0][inner]
                    for d in range(1, slab_count):
                        box = jnp.where(away == d, pools[d][inner], box)
                else:
                    away = lax.rem(slab - slab_position + halo_depth + slab_count, slab_count)
                    box = pools[0][away * group_size + lax.rem(partner, group_size)]
                box = box.astype(jnp.float32)
                flat = shift[1] * box_edge + shift[2]
                flat = lax.rem(RADIX * plane - flat, plane)
                box = pltpu.roll(box, flat, 1)
                box = pltpu.roll(box, lax.rem(RADIX * box_edge - shift[0], box_edge), 0)
                a_src = a_ids + shift[0]
                b_src = b_ids + shift[1]
                c_src = c_ids + shift[2]
                in_a = (a_src >= 0) & (a_src < box_edge) & usable
                in_bc = (b_src >= 0) & (b_src < box_edge) & (c_src >= 0) & (c_src < box_edge)
                weight = in_a.astype(jnp.float32) * in_bc.astype(jnp.float32)
                moved_box[p] = box * weight
            density = (moved_box[...] * centre[None]).reshape(rows, plane)
            x0, x1, x2, x3 = (density[:, t * tile:(t + 1) * tile] for t in range(RADIX))
            even, odd = x0 + x2, x1 + x3
            tables = [(plane_tab[0, q], plane_tab[1, q]) for q in range(RADIX - 1)]
            y0 = product(split(even + odd), tables[0], NN)
            y2 = product(split(even - odd), tables[2], NN)
            uv = product(split(jnp.concatenate([x0 - x2, x1 - x3], axis=0)), tables[1], NN)
            y1_re = uv[:rows, :tile] + uv[rows:, tile:]
            y1_im = uv[:rows, tile:] - uv[rows:, :tile]
            spectrum = jnp.concatenate(
                [
                    jnp.concatenate([y0[:, :tile], y1_re, y2[:, :tile]], axis=1),
                    jnp.concatenate([y0[:, tile:], y1_im, y2[:, tile:]], axis=1),
                ],
                axis=0,
            )
            spectrum = product((edge_tab[0, 0], edge_tab[1, 0]), split(spectrum), NN)
            width = spectrum.shape[1]
            spectrum = spectrum.reshape(2 * PB, box_edge, width) * filters[...][None]
            spectrum = spectrum.reshape(2 * rows, width)
            spectrum = product((edge_tab[0, 1], edge_tab[1, 1]), split(spectrum), NN)
            re, im = spectrum[:rows], spectrum[rows:]
            pick = lambda part, q: part[:, q * tile:(q + 1) * tile]
            z0 = product(split(jnp.concatenate([pick(re, 0), pick(im, 0)], axis=1)), tables[0], NT)
            z2 = product(split(jnp.concatenate([pick(re, 2), pick(im, 2)], axis=1)), tables[2], NT)
            both = jnp.concatenate(
                [
                    jnp.concatenate([pick(re, 1), pick(im, 1)], axis=1),
                    jnp.concatenate([pick(im, 1), -pick(re, 1)], axis=1),
                ],
                axis=0,
            )
            z1 = product(split(both), tables[1], NT)
            z1_re, z1_im = z1[:rows], z1[rows:]
            even, odd = z0 + z2, z0 - z2
            parts = (even + z1_re, odd - z1_im, even - z1_re, odd + z1_im)
            for t in range(RADIX):
                span = pl.ds(t * tile, tile)
                term = parts[t].reshape(PB, box_edge, tile) * moved_box[:, :, span]
                out[held, span] = out[held, span] - jnp.sum(term, axis=0)
            return carry

        lax.fori_loop(0, (filled + PB - 1) // PB, block, 0)
        summed = jnp.sum(out[held] * centre, axis=0, keepdims=True)
        total = total + jnp.sum(summed, axis=1, keepdims=True)
    out[pl.ds(own_count * box_edge, 8)] = jnp.broadcast_to(total, (8, plane))


def body(orbitals, corners, partners, kernel):
    own_count, box_edge, plane = orbitals.shape
    slab_count = lax.axis_size("slab")
    orb_count = lax.axis_size("orb")
    halo_depth = (ZDEV + box_edge - 2) // ZDEV
    rep_count = lax.axis_size("rep")
    turned = slab_count <= 2 * halo_depth + 1 and orb_count == rep_count
    if turned:
        pools = turned_boxes(orbitals)
    else:
        gathered = lax.all_gather(orbitals, "orb", axis=0, tiled=True)
        lower = [gathered]
        upper = [gathered]
        for _ in range(halo_depth):
            lower.append(passed_along(lower[-1], "slab", 1))
            upper.append(passed_along(upper[-1], "slab", -1))
        pools = [jnp.concatenate(lower[::-1] + upper[1:], axis=0)]
    plane_tab, edge_tab = fourier_tables(box_edge)
    smem = pl.BlockSpec(memory_space=pltpu.SMEM)
    vmem = pl.BlockSpec(memory_space=pltpu.VMEM)
    sums = pl.pallas_call(
        functools.partial(
            pair_kernel,
            slab_count=slab_count,
            orb_count=orb_count,
            rep_count=rep_count,
            halo_depth=halo_depth,
            turned=turned,
        ),
        in_specs=[smem, smem, vmem, vmem, vmem, vmem] + [vmem] * len(pools),
        out_specs=vmem,
        out_shape=jax.ShapeDtypeStruct((own_count * box_edge + 8, plane), jnp.float32),
        scratch_shapes=[
            pltpu.VMEM((PB, box_edge, plane), jnp.float32),
            pltpu.VMEM((box_edge, (RADIX - 1) * plane // RADIX), jnp.float32),
            pltpu.SMEM((partners.shape[1] + 1,), jnp.int32),
        ],
        name="pairs",
    )(partners, corners.T, orbitals, kernel, plane_tab, edge_tab, *pools)
    held = own_count * box_edge
    other = lax.ppermute(sums, "rep", [(i, i ^ 1) for i in range(rep_count)])
    energy = sums[held:, :128] + other[held:, :128]
    exchange = (sums[:held] + other[:held]).reshape(own_count, box_edge, plane)
    energy_all = swapped_sum(energy, ("orb", "slab"))[0, :1]
    orbital_total = own_count * slab_count * orb_count
    return exchange, energy_all / (2.0 * orbital_total * box_edge**3)


def solution(mesh):
    in_specs = (
        P(("grp", "slab", "orb"), None, None),
        P("grp", None),
        P(("grp", "slab", "orb"), None),
        P(),
    )
    out_specs = (P(("grp", "slab", "orb"), None, None), P("grp"))
    return jax.shard_map(body, mesh=mesh, in_specs=in_specs, out_specs=out_specs, check_vma=False)
```
